32 devices in a mesh: tm: 8 (over z, x), col: 4 (over y, core).
Axes of the slice: x: 2, y: 2, z: 4, core: 2. Of those that a mesh axis runs over, the one named last changes fastest.
Arguments:
- near_prop: bfloat16 [16, 2, 512, 512], P('tm', None, None, 'col'), may hold values from -0.1875 to 0.1875
- far_prop: bfloat16 [16, 2, 512, 512], P('tm', None, None, 'col'), may hold values from -0.1875 to 0.1875
- meson: bfloat16 [16, 2, 512, 512], P('tm', None, None, 'col'), may hold values from -6 to 6
Outputs:
- blocks: float32 [16, 2, 512, 512], P('tm', None, None, 'col')
The draws below stay inside these ranges and needn't reach their ends.
All inputs are finite; a program needn't handle non-finite values.
Results may differ from the reference program's by a relative error of at most 0.0035.
Values may be sent and summed in bfloat16 or wider, within the bound.
A program may use at most 64 MiB of HBM per device.

```python
import jax
import jax.numpy as jnp
from jax import lax

NO = 512
TIMES = 16
SEP_NEAR = 2
SEP_FAR = 6


def block_levels(stream_key, shape, shards, least, high):
    level = 1.0
    for dim, blocks in shards:
        heights = jax.random.uniform(jax.random.fold_in(jax.random.fold_in(stream_key, 6), dim), (blocks,), jnp.float32, least / len(shards), high / len(shards))
        level = level * jnp.repeat(jnp.exp(heights), shape[dim] // blocks).reshape((-1,) + (1,) * (len(shape) - 1 - dim))
    return level


def gaussian(key, shape, scale, bound, shards=(), dtype=jnp.bfloat16):
    values = jax.random.normal(key, shape, jnp.float32) * scale
    if len(shards) > 0:
        values = block_levels(key, shape, shards, -0.22, 0.18) * values
    return jnp.clip(values, min=-bound, max=bound).astype(dtype)


def setup_inputs(seed: int = 0) -> dict:
    streams_of = jax.random.split(jax.random.key(seed), 4)
    near_prop = gaussian(streams_of[0], (TIMES, 2, NO, NO), (2 * NO) ** -0.5, 0.1875, ((0, 8), (3, 4)))
    far_prop = gaussian(streams_of[1], (TIMES, 2, NO, NO), (2 * NO) ** -0.5, 0.1875, ((0, 8), (3, 4)))
    meson = gaussian(streams_of[2], (TIMES, 2, NO, NO), 1.0, 6.0, ((0, 8), (3, 4)))
    return dict(near_prop=near_prop, far_prop=far_prop, meson=meson)


def complex_product(left, right):
    real_part = jnp.einsum("tik,tkj->tij", left[:, 0], right[:, 0], precision=lax.Precision.HIGHEST) - jnp.einsum("tik,tkj->tij", left[:, 1], right[:, 1], precision=lax.Precision.HIGHEST)
    imag_part = jnp.einsum("tik,tkj->tij", left[:, 0], right[:, 1], precision=lax.Precision.HIGHEST) + jnp.einsum("tik,tkj->tij", left[:, 1], right[:, 0], precision=lax.Precision.HIGHEST)
    return jnp.stack([real_part, imag_part], axis=1)


def to_half(value):
    rounded = value.astype(jnp.bfloat16)
    rounded = lax.optimization_barrier(rounded)
    return rounded.astype(jnp.float32)


def gamma_adjoint(perambulator):
    order = perambulator.shape[2]
    signs = jnp.where(jnp.arange(order) < order // 2, 1.0, -1.0).astype(jnp.float32)
    both_signs = signs[:, None] * signs[None, :]
    conjugate = jnp.stack([perambulator[:, 0], -perambulator[:, 1]], axis=1)
    return jnp.swapaxes(conjugate, 2, 3) * both_signs


def reference(near_prop, far_prop, meson):
    meson_full = meson.astype(jnp.float32)
    total = jnp.zeros(meson.shape, jnp.float32)
    for separation, perambulator in ((SEP_NEAR, near_prop), (SEP_FAR, far_prop)):
        prop_full = perambulator.astype(jnp.float32)
        adjoint = gamma_adjoint(prop_full)
        shifted = jnp.roll(meson_full, -separation, axis=0)
        ahead = to_half(complex_product(shifted, prop_full))
        total = total + complex_product(adjoint, ahead)
        inner = to_half(complex_product(meson_full, adjoint))
        backward = to_half(complex_product(prop_full, inner))
        total = total + jnp.roll(backward, separation, axis=0)
    return total
```

```python
import functools

import jax
import jax.numpy as jnp
from jax import lax
from jax.experimental import pallas as pl
from jax.experimental.pallas import tpu as pltpu
from jax.sharding import PartitionSpec as P

MESH = pl.DeviceIdType.MESH
BF16 = jnp.bfloat16
F32 = jnp.float32


def left_form(real, imag):
    top = jnp.concatenate([real, -imag], axis=1)
    low = jnp.concatenate([imag, real], axis=1)
    return jnp.concatenate([top, low], axis=0)


def from_blocks(blocks):
    count = blocks.shape[0]
    real = jnp.concatenate([blocks[j, 0] for j in range(count)], axis=1)
    imag = jnp.concatenate([blocks[j, 1] for j in range(count)], axis=1)
    return left_form(real, imag)


def kernel(
    n_tm, n_col, near, far, meson, out,
    p_in, m_in, a_in, b_out, f_out, b_in, f_in, p_nat, t_nat, i_nat, a_nat,
    p_sem, m_sem, a_sem, b_sem, f_sem, p_send, m_send, b_send, f_send,
):
    order = near.shape[2]
    width = near.shape[3]
    half = order // 2
    tm = lax.axis_index("tm")
    me = lax.axis_index("col")
    y, c = me // 2, me % 2
    step_near, step_far = n_tm // 8, 3 * n_tm // 8
    partner = 2 * y + 1 - c
    across = 2 * (1 - y) + c

    def shifted(by):
        return lax.rem(tm + by + n_tm, n_tm)

    barrier = pltpu.get_barrier_semaphore()
    for d in range(1, n_col):
        pl.semaphore_signal(barrier, inc=1, device_id=(tm, lax.rem(me + d, n_col)), device_id_type=MESH)
    for by in (step_near, -step_near, step_far, -step_far):
        for j in range(n_col):
            pl.semaphore_signal(barrier, inc=1, device_id=(shifted(by), j), device_id_type=MESH)
    pl.semaphore_wait(barrier, n_col - 1 + 4 * n_col)

    def remote(src, dst, send, recv, device):
        return pltpu.make_async_remote_copy(
            src_ref=src, dst_ref=dst, send_sem=send, recv_sem=recv, device_id=device, device_id_type=MESH
        )

    behind_near = (shifted(-step_near), 2 * y)
    behind_far = (shifted(-step_far), 2 * y + 1)

    cross = remote(meson.at[1 - y], m_in.at[me], m_send.at[0], m_sem.at[me], (tm, across))
    cross.start()
    own = [
        remote(meson.at[y], a_in.at[me], m_send.at[1], a_sem.at[me], behind_near),
        remote(meson.at[y], a_in.at[me], m_send.at[2], a_sem.at[me], behind_far),
        remote(meson.at[y], m_in.at[me], m_send.at[3], m_sem.at[me], (tm, partner)),
    ]
    for copy in own:
        copy.start()
    pltpu.make_async_copy(meson.at[y], m_in.at[me], m_sem.at[me]).start()

    def p_copy(target):
        src = (near, far)[target % 2].at[target // 2]
        return remote(src, p_in.at[me], p_send.at[target], p_sem.at[me], (tm, target))

    for target in range(n_col):
        @pl.when(me != target)
        def _():
            p_copy(target).start()

        @pl.when(me == target)
        def _():
            src = (near, far)[target % 2].at[target // 2]
            pltpu.make_async_copy(src, p_in.at[me], p_sem.at[me]).start()

    def arrived(buf, sem, j):
        pltpu.make_async_copy(buf.at[j], buf.at[j], sem.at[j]).wait()

    arrived(m_in, m_sem, across)
    passed = [
        remote(m_in.at[across], m_in.at[across], m_send.at[4], m_sem.at[across], (tm, partner)),
        remote(m_in.at[across], a_in.at[across], m_send.at[5], a_sem.at[across], behind_near),
        remote(m_in.at[across], a_in.at[across], m_send.at[6], a_sem.at[across], behind_far),
    ]
    for copy in passed:
        copy.start()

    for j in range(n_col):
        arrived(p_in, p_sem, j)
    rows = lax.broadcasted_iota(jnp.int32, (order, width), 0)
    for j in range(n_col):
        columns = lax.broadcasted_iota(jnp.int32, (order, width), 1) + j * width
        sign = jnp.where((rows < half) == (columns < half), 1.0, -1.0).astype(F32)
        for part in range(2):
            block = p_in[j, part]
            p_nat[part * order:(part + 1) * order, j * width:(j + 1) * width] = block
            signed = block.astype(F32) * (sign if part == 0 else -sign)
            turned = jnp.transpose(signed).astype(BF16)
            t_nat[part * order + j * width:part * order + (j + 1) * width, :] = turned

    tile = 2 * width

    def product(left, right, store):
        def step(i, carry):
            at = pl.ds(pl.multiple_of(i * tile, tile), tile)
            store(i, at, jnp.dot(left(), right[:, at], preferred_element_type=F32).astype(BF16))
            return carry

        lax.fori_loop(0, order // tile, step, 0)

    def natural(ref):
        def store(i, at, value):
            ref[:, at] = value
        return store

    def blocked(ref):
        def store(i, at, value):
            for k in range(2):
                for part in range(2):
                    ref[2 * i + k, part] = value[part * order:(part + 1) * order, k * width:(k + 1) * width]
        return store

    for d in range(1, n_col):
        arrived(m_in, m_sem, lax.rem(across + d, n_col))

    product(lambda: from_blocks(m_in), t_nat, natural(i_nat))
    product(lambda: from_blocks(p_in), i_nat, blocked(b_out))
    home = jnp.where(c == 0, shifted(step_near), shifted(step_far))
    b_copies = [
        remote(b_out.at[j], b_in.at[c, y], b_send.at[j], b_sem.at[c, y], (home, j)) for j in range(n_col)
    ]
    for copy in b_copies:
        copy.start()

    for j in range(n_col):
        arrived(a_in, a_sem, j)
    product(lambda: from_blocks(a_in), p_nat, natural(a_nat))
    product(lambda: left_form(t_nat[:order, :], t_nat[order:, :]), a_nat, blocked(f_out))

    def f_copy(target):
        return remote(f_out.at[target], f_in.at[c, y], f_send.at[target], f_sem.at[c, y], (tm, target))

    for target in range(n_col):
        @pl.when(me != target)
        def _():
            f_copy(target).start()

        @pl.when(me == target)
        def _():
            pltpu.make_async_copy(f_out.at[target], f_in.at[c, y], f_sem.at[c, y]).start()

    for s in range(2):
        for p in range(2):
            for buf, sem in ((f_in, f_sem), (b_in, b_sem)):
                pltpu.make_async_copy(buf.at[s, p], buf.at[s, p], sem.at[s, p]).wait()
    for p in range(2):
        for part in range(2):
            out[p, part] = (
                f_in[0, p, part].astype(F32) + f_in[1, p, part].astype(F32)
                + b_in[0, p, part].astype(F32) + b_in[1, p, part].astype(F32)
            )

    cross.wait_send()
    for copy in own + passed + b_copies:
        copy.wait_send()
    for target in range(n_col):
        @pl.when(me != target)
        def _():
            p_copy(target).wait_send()
            f_copy(target).wait_send()


def shards(n_tm, n_col, near_prop, far_prop, meson):
    slices, parts, order, width = meson.shape
    blocks = pltpu.VMEM((n_col, parts, order, width), BF16)
    homes = pltpu.VMEM((2, slices, parts, order, width), BF16)
    whole = pltpu.VMEM((parts * order, order), BF16)
    dma = pltpu.SemaphoreType.DMA
    return pl.pallas_call(
        functools.partial(kernel, n_tm, n_col),
        out_shape=jax.ShapeDtypeStruct(meson.shape, F32),
        in_specs=[pl.BlockSpec(memory_space=pl.ANY)] * 3,
        out_specs=pl.BlockSpec(memory_space=pltpu.VMEM),
        scratch_shapes=[
            blocks, blocks, blocks, blocks, blocks, homes, homes, whole, whole, whole, whole,
            dma((n_col,)), dma((n_col,)), dma((n_col,)), dma((2, slices)), dma((2, slices)),
            dma((n_col,)), dma((7,)), dma((n_col,)), dma((n_col,)),
        ],
        compiler_params=pltpu.CompilerParams(
            collective_id=0, has_side_effects=True, vmem_limit_bytes=56 * 1024 * 1024
        ),
    )(near_prop, far_prop, meson)


def solution(mesh):
    spec = P("tm", None, None, "col")
    body = functools.partial(shards, mesh.shape["tm"], mesh.shape["col"])
    return jax.shard_map(body, mesh=mesh, in_specs=(spec, spec, spec), out_specs=spec, check_vma=False)
```

```python
import functools

import jax
import jax.numpy as jnp
from jax import lax
from jax.experimental import pallas as pl
from jax.experimental.pallas import tpu as pltpu
from jax.sharding import PartitionSpec as P

MESH = pl.DeviceIdType.MESH
BF16 = jnp.bfloat16
F32 = jnp.float32


def left_form(real, imag):
    top = jnp.concatenate([real, -imag], axis=1)
    low = jnp.concatenate([imag, real], axis=1)
    return jnp.concatenate([top, low], axis=0)


def from_blocks(blocks):
    count = blocks.shape[0]
    real = jnp.concatenate([blocks[j, 0] for j in range(count)], axis=1)
    imag = jnp.concatenate([blocks[j, 1] for j in range(count)], axis=1)
    return left_form(real, imag)


def kernel(
    n_tm, n_col, near, far, meson, f_in, b_in,
    p_in, m_in, a_in, b_out, f_out, ra_in, rb_in, p_nat, t_nat,
    p_sem, m_sem, a_sem, b_sem, f_sem, ra_sem, rb_sem, p_send, m_send, b_send, f_send, r_send,
):
    order = near.shape[2]
    width = near.shape[3]
    half = order // 2
    tm = lax.axis_index("tm")
    me = lax.axis_index("col")
    y, c = me // 2, me % 2
    step_near, step_far = n_tm // 8, 3 * n_tm // 8
    partner = 2 * y + 1 - c
    across = 2 * (1 - y) + c
    beyond = 2 * (1 - y) + 1 - c
    relayed = step_near % 2 == 1
    at_x0 = tm % 2 == 0
    tile = 2 * width

    def shifted(by):
        return lax.rem(tm + by + n_tm, n_tm)

    barrier = pltpu.get_barrier_semaphore()
    steps = (step_near, step_far) + ((2 * step_near,) if relayed else ())
    for d in range(1, n_col):
        pl.semaphore_signal(barrier, inc=1, device_id=(tm, lax.rem(me + d, n_col)), device_id_type=MESH)
    for step in steps:
        for by in (step, -step):
            for j in range(n_col):
                pl.semaphore_signal(barrier, inc=1, device_id=(shifted(by), j), device_id_type=MESH)
    pl.semaphore_wait(barrier, n_col - 1 + 2 * len(steps) * n_col)

    def remote(src, dst, send, recv, device):
        return pltpu.make_async_remote_copy(
            src_ref=src, dst_ref=dst, send_sem=send, recv_sem=recv, device_id=device, device_id_type=MESH
        )

    def by_x(at_0, at_1):
        if relayed:
            pl.when(at_x0)(at_0)
            pl.when(jnp.logical_not(at_x0))(at_1)
        else:
            at_1()

    def arrived(buf, sem, j):
        pltpu.make_async_copy(buf.at[j], buf.at[j], sem.at[j]).wait()

    behind_near = (shifted(-step_near), 2 * y)
    behind_far = (shifted(-step_far), 2 * y + 1)

    def ahead_near(src, j, k):
        return remote(src, a_in.at[j], m_send.at[k], a_sem.at[j], behind_near)

    def ahead_near_first(src, k):
        return remote(src, ra_in.at[k], m_send.at[k], ra_sem.at[k], (shifted(-2 * step_near), me))

    def ahead_near_second(k):
        j = (me, across)[k]
        return remote(ra_in.at[k], a_in.at[j], r_send.at[k], a_sem.at[j], behind_mid)

    behind_mid = (shifted(step_near), 2 * y)

    def ahead_far(src, j, k):
        return remote(src, a_in.at[j], m_send.at[2 + k], a_sem.at[j], behind_far)

    def to_partner(src, j, k):
        return remote(src, m_in.at[j], m_send.at[4 + k], m_sem.at[j], (tm, partner))

    def spread(src, j, k):
        by_x(lambda: ahead_near_first(src, k).start(), lambda: ahead_near(src, j, k).start())
        ahead_far(src, j, k).start()
        to_partner(src, j, k).start()

    def p_copy(target):
        src = (near, far)[target % 2].at[target // 2]
        return remote(src, p_in.at[me], p_send.at[target], p_sem.at[me], (tm, target))

    cross = remote(meson.at[1 - y], m_in.at[me], m_send.at[6], m_sem.at[me], (tm, across))
    cross.start()
    spread(meson.at[y], me, 0)
    pltpu.make_async_copy(meson.at[y], m_in.at[me], m_sem.at[me]).start()
    for target in range(n_col):
        @pl.when(me != target)
        def _():
            p_copy(target).start()

        @pl.when(me == target)
        def _():
            src = (near, far)[target % 2].at[target // 2]
            pltpu.make_async_copy(src, p_in.at[me], p_sem.at[me]).start()

    rows = lax.broadcasted_iota(jnp.int32, (order, width), 0)

    def prepare(j):
        arrived(p_in, p_sem, j)
        first = pl.multiple_of(j * width, width)
        columns = lax.broadcasted_iota(jnp.int32, (order, width), 1) + j * width
        sign = jnp.where((rows < half) == (columns < half), 1.0, -1.0).astype(F32)
        for part in range(2):
            block = p_in[j, part]
            p_nat[part * order:(part + 1) * order, pl.ds(first, width)] = block
            signed = block.astype(F32) * (sign if part == 0 else -sign)
            t_nat[pl.ds(part * order + first, width), :] = jnp.transpose(signed).astype(BF16)

    prepare(me)
    prepare(partner)
    arrived(m_in, m_sem, across)
    spread(m_in.at[across], across, 1)
    if relayed:
        @pl.when(at_x0)
        def _():
            for k in range(2):
                arrived(ra_in, ra_sem, k)
                ahead_near_second(k).start()
    prepare(across)
    prepare(beyond)
    for j in (me, partner, beyond):
        arrived(m_in, m_sem, j)

    def product(left, right):
        return jnp.dot(left, right, preferred_element_type=F32).astype(BF16)

    def store(ref, i, value):
        for k in range(2):
            for part in range(2):
                ref[2 * i + k, part] = value[part * order:(part + 1) * order, k * width:(k + 1) * width]

    ahead_by = jnp.where(c == 0, step_near, step_far)
    first_by = jnp.where(c == 0, 2 * step_near, step_far)

    def b_copy(j):
        return remote(b_out.at[j], b_in.at[c, y], b_send.at[j], b_sem.at[c, y], (shifted(ahead_by), j))

    def b_first(j):
        return remote(b_out.at[j], rb_in.at[y], b_send.at[j], rb_sem.at[y], (shifted(2 * step_near), j))

    def b_second(p):
        return remote(rb_in.at[p], b_in.at[0, p], r_send.at[2 + p], b_sem.at[0, p], (shifted(-step_near), me))

    goes_first = jnp.logical_and(c == 0, jnp.logical_not(at_x0))

    def b_send_all(i, act):
        for j in (2 * i, 2 * i + 1):
            if relayed:
                @pl.when(goes_first)
                def _():
                    act(b_first(j))

                @pl.when(jnp.logical_not(goes_first))
                def _():
                    act(b_copy(j))
            else:
                act(b_copy(j))

    for i in range(order // tile):
        at = pl.ds(i * tile, tile)
        inner = product(from_blocks(m_in), t_nat[:, at])
        store(b_out, i, product(from_blocks(p_in), inner))
        b_send_all(i, lambda copy: copy.start())

    for j in range(n_col):
        arrived(a_in, a_sem, j)

    def f_copy(target):
        return remote(f_out.at[target], f_in.at[c, y], f_send.at[target], f_sem.at[c, y], (tm, target))

    for i in range(order // tile):
        at = pl.ds(i * tile, tile)
        ahead = product(from_blocks(a_in), p_nat[:, at])
        store(f_out, i, product(left_form(t_nat[:order, :], t_nat[order:, :]), ahead))
        for target in (2 * i, 2 * i + 1):
            @pl.when(me != target)
            def _():
                f_copy(target).start()

            @pl.when(me == target)
            def _():
                pltpu.make_async_copy(f_out.at[target], f_in.at[c, y], f_sem.at[c, y]).start()

    if relayed:
        @pl.when(jnp.logical_not(at_x0))
        def _():
            for p in (y, 1 - y):
                arrived(rb_in, rb_sem, p)
                b_second(p).start()

    for s in range(2):
        for p in range(2):
            for buf, sem in ((f_in, f_sem), (b_in, b_sem)):
                pltpu.make_async_copy(buf.at[s, p], buf.at[s, p], sem.at[s, p]).wait()

    cross.wait_send()
    for k in range(2):
        src, j = ((meson.at[y], me), (m_in.at[across], across))[k]
        by_x(lambda: ahead_near_first(src, k).wait_send(), lambda: ahead_near(src, j, k).wait_send())
        ahead_far(src, j, k).wait_send()
        to_partner(src, j, k).wait_send()
    if relayed:
        @pl.when(at_x0)
        def _():
            for k in range(2):
                ahead_near_second(k).wait_send()

        @pl.when(jnp.logical_not(at_x0))
        def _():
            for p in (y, 1 - y):
                b_second(p).wait_send()
    for i in range(order // tile):
        b_send_all(i, lambda copy: copy.wait_send())
    for target in range(n_col):
        @pl.when(me != target)
        def _():
            p_copy(target).wait_send()
            f_copy(target).wait_send()


def shards(n_tm, n_col, near_prop, far_prop, meson):
    slices, parts, order, width = meson.shape
    blocks = pltpu.VMEM((n_col, parts, order, width), BF16)
    pair = pltpu.VMEM((2, parts, order, width), BF16)
    whole = pltpu.VMEM((parts * order, order), BF16)
    home = jax.ShapeDtypeStruct((2, slices, parts, order, width), BF16)
    dma = pltpu.SemaphoreType.DMA
    forward, backward = pl.pallas_call(
        functools.partial(kernel, n_tm, n_col),
        out_shape=(home, home),
        in_specs=[pl.BlockSpec(memory_space=pl.ANY)] * 3,
        out_specs=[pl.BlockSpec(memory_space=pl.ANY)] * 2,
        scratch_shapes=[
            blocks, blocks, blocks, blocks, blocks, pair, pair, whole, whole,
            dma((n_col,)), dma((n_col,)), dma((n_col,)), dma((2, slices)), dma((2, slices)), dma((2,)), dma((2,)),
            dma((n_col,)), dma((7,)), dma((n_col,)), dma((n_col,)), dma((4,)),
        ],
        compiler_params=pltpu.CompilerParams(
            collective_id=0, has_side_effects=True, vmem_limit_bytes=56 * 1024 * 1024
        ),
    )(near_prop, far_prop, meson)
    forward, backward = forward.astype(F32), backward.astype(F32)
    return forward[0] + forward[1] + backward[0] + backward[1]


def solution(mesh):
    spec = P("tm", None, None, "col")
    body = functools.partial(shards, mesh.shape["tm"], mesh.shape["col"])
    return jax.shard_map(body, mesh=mesh, in_specs=(spec, spec, spec), out_specs=spec, check_vma=False)
```

```python
import functools

import jax
import jax.numpy as jnp
from jax import lax
from jax.experimental import pallas as pl
from jax.experimental.pallas import tpu as pltpu
from jax.sharding import PartitionSpec as P

MESH = pl.DeviceIdType.MESH
BF16 = jnp.bfloat16
F32 = jnp.float32


def left_form(real, imag):
    top = jnp.concatenate([real, -imag], axis=1)
    low = jnp.concatenate([imag, real], axis=1)
    return jnp.concatenate([top, low], axis=0)


def from_blocks(blocks):
    count = blocks.shape[0]
    real = jnp.concatenate([blocks[j, 0] for j in range(count)], axis=1)
    imag = jnp.concatenate([blocks[j, 1] for j in range(count)], axis=1)
    return left_form(real, imag)


def kernel(
    n_tm, n_col, near, far, meson, f_in, b_in,
    p_in, m_in, a_in, b_out, f_out, ra_in, rb_in, p_nat, t_nat,
    p_sem, m_sem, a_sem, b_sem, f_sem, ra_sem, rb_sem, p_send, m_send, b_send, f_send, r_send,
):
    order = near.shape[2]
    width = near.shape[3]
    half = order // 2
    tm = lax.axis_index("tm")
    me = lax.axis_index("col")
    y, c = me // 2, me % 2
    step_near, step_far = n_tm // 8, 3 * n_tm // 8
    partner = 2 * y + 1 - c
    across = 2 * (1 - y) + c
    beyond = 2 * (1 - y) + 1 - c
    relayed = step_near % 2 == 1
    at_x0, at_x1 = tm % 2 == 0, tm % 2 == 1
    tile = 2 * width

    def shifted(by):
        return lax.rem(tm + by + n_tm, n_tm)

    barrier = pltpu.get_barrier_semaphore()
    steps = (step_near, step_far) + ((2 * step_near,) if relayed else ())
    for d in range(1, n_col):
        pl.semaphore_signal(barrier, inc=1, device_id=(tm, lax.rem(me + d, n_col)), device_id_type=MESH)
    for step in steps:
        for by in (step, -step):
            for j in range(n_col):
                pl.semaphore_signal(barrier, inc=1, device_id=(shifted(by), j), device_id_type=MESH)
    pl.semaphore_wait(barrier, n_col - 1 + 2 * len(steps) * n_col)

    def remote(src, dst, send, recv, device):
        return pltpu.make_async_remote_copy(
            src_ref=src, dst_ref=dst, send_sem=send, recv_sem=recv, device_id=device, device_id_type=MESH
        )

    def by_x(at_0, at_1):
        if relayed:
            pl.when(at_x0)(at_0)
            pl.when(at_x1)(at_1)
        else:
            at_1()

    def arrived(buf, sem, j):
        pltpu.make_async_copy(buf.at[j], buf.at[j], sem.at[j]).wait()

    behind_near = (shifted(-step_near), 2 * y)
    behind_far = (shifted(-step_far), 2 * y + 1)

    def ahead_near(src, j, k):
        return remote(src, a_in.at[j], m_send.at[k], a_sem.at[j], behind_near)

    def ahead_near_first(src, k):
        return remote(src, ra_in.at[k], m_send.at[k], ra_sem.at[k], (shifted(step_near), me))

    def ahead_near_second(k):
        j = (me, across)[k]
        return remote(ra_in.at[k], a_in.at[j], r_send.at[k], a_sem.at[j], behind_mid)

    behind_mid = (shifted(-2 * step_near), 2 * y)

    def ahead_far(src, j, k):
        return remote(src, a_in.at[j], m_send.at[2 + k], a_sem.at[j], behind_far)

    def to_partner(src, j, k):
        return remote(src, m_in.at[j], m_send.at[4 + k], m_sem.at[j], (tm, partner))

    def spread(src, j, k):
        by_x(lambda: ahead_near_first(src, k).start(), lambda: ahead_near(src, j, k).start())
        ahead_far(src, j, k).start()
        to_partner(src, j, k).start()

    def p_copy(target):
        src = (near, far)[target % 2].at[target // 2]
        return remote(src, p_in.at[me], p_send.at[target], p_sem.at[me], (tm, target))

    cross = remote(meson.at[1 - y], m_in.at[me], m_send.at[6], m_sem.at[me], (tm, across))
    cross.start()
    spread(meson.at[y], me, 0)
    pltpu.make_async_copy(meson.at[y], m_in.at[me], m_sem.at[me]).start()
    for target in range(n_col):
        @pl.when(me != target)
        def _():
            p_copy(target).start()

        @pl.when(me == target)
        def _():
            src = (near, far)[target % 2].at[target // 2]
            pltpu.make_async_copy(src, p_in.at[me], p_sem.at[me]).start()

    rows = lax.broadcasted_iota(jnp.int32, (order, width), 0)

    def prepare(j):
        arrived(p_in, p_sem, j)
        first = pl.multiple_of(j * width, width)
        columns = lax.broadcasted_iota(jnp.int32, (order, width), 1) + j * width
        sign = jnp.where((rows < half) == (columns < half), 1.0, -1.0).astype(F32)
        for part in range(2):
            block = p_in[j, part]
            p_nat[part * order:(part + 1) * order, pl.ds(first, width)] = block
            signed = block.astype(F32) * (sign if part == 0 else -sign)
            t_nat[pl.ds(part * order + first, width), :] = jnp.transpose(signed).astype(BF16)

    prepare(me)
    prepare(partner)
    arrived(m_in, m_sem, across)
    spread(m_in.at[across], across, 1)
    if relayed:
        @pl.when(at_x1)
        def _():
            for k in range(2):
                arrived(ra_in, ra_sem, k)
                ahead_near_second(k).start()
    prepare(across)
    prepare(beyond)
    for j in (me, partner, beyond):
        arrived(m_in, m_sem, j)

    def product(left, right):
        return jnp.dot(left, right, preferred_element_type=F32).astype(BF16)

    def store(ref, i, value):
        for k in range(2):
            for part in range(2):
                ref[2 * i + k, part] = value[part * order:(part + 1) * order, k * width:(k + 1) * width]

    ahead_by = jnp.where(c == 0, step_near, step_far)

    def b_copy(j):
        return remote(b_out.at[j], b_in.at[c, y], b_send.at[j], b_sem.at[c, y], (shifted(ahead_by), j))

    def b_first(j):
        return remote(b_out.at[j], rb_in.at[y], b_send.at[j], rb_sem.at[y], (shifted(-step_near), j))

    def b_second(p):
        return remote(rb_in.at[p], b_in.at[0, p], r_send.at[2 + p], b_sem.at[0, p], (shifted(2 * step_near), me))

    goes_first = jnp.logical_and(c == 0, at_x1)

    def b_send_all(i, act):
        for j in (2 * i, 2 * i + 1):
            if relayed:
                @pl.when(goes_first)
                def _():
                    act(b_first(j))

                @pl.when(jnp.logical_not(goes_first))
                def _():
                    act(b_copy(j))
            else:
                act(b_copy(j))

    for i in range(order // tile):
        at = pl.ds(i * tile, tile)
        inner = product(from_blocks(m_in), t_nat[:, at])
        store(b_out, i, product(from_blocks(p_in), inner))
        b_send_all(i, lambda copy: copy.start())

    for j in range(n_col):
        arrived(a_in, a_sem, j)

    def f_copy(target):
        return remote(f_out.at[target], f_in.at[c, y], f_send.at[target], f_sem.at[c, y], (tm, target))

    for i in range(order // tile):
        at = pl.ds(i * tile, tile)
        ahead = product(from_blocks(a_in), p_nat[:, at])
        store(f_out, i, product(left_form(t_nat[:order, :], t_nat[order:, :]), ahead))
        for target in (2 * i, 2 * i + 1):
            @pl.when(me != target)
            def _():
                f_copy(target).start()

            @pl.when(me == target)
            def _():
                pltpu.make_async_copy(f_out.at[target], f_in.at[c, y], f_sem.at[c, y]).start()

    if relayed:
        @pl.when(at_x0)
        def _():
            for p in (y, 1 - y):
                arrived(rb_in, rb_sem, p)
                b_second(p).start()

    for s in range(2):
        for p in range(2):
            for buf, sem in ((f_in, f_sem), (b_in, b_sem)):
                pltpu.make_async_copy(buf.at[s, p], buf.at[s, p], sem.at[s, p]).wait()

    cross.wait_send()
    for k in range(2):
        src, j = ((meson.at[y], me), (m_in.at[across], across))[k]
        by_x(lambda: ahead_near_first(src, k).wait_send(), lambda: ahead_near(src, j, k).wait_send())
        ahead_far(src, j, k).wait_send()
        to_partner(src, j, k).wait_send()
    if relayed:
        @pl.when(at_x1)
        def _():
            for k in range(2):
                ahead_near_second(k).wait_send()

        @pl.when(at_x0)
        def _():
            for p in (y, 1 - y):
                b_second(p).wait_send()
    for i in range(order // tile):
        b_send_all(i, lambda copy: copy.wait_send())
    for target in range(n_col):
        @pl.when(me != target)
        def _():
            p_copy(target).wait_send()
            f_copy(target).wait_send()


def shards(n_tm, n_col, near_prop, far_prop, meson):
    slices, parts, order, width = meson.shape
    blocks = pltpu.VMEM((n_col, parts, order, width), BF16)
    pair = pltpu.VMEM((2, parts, order, width), BF16)
    whole = pltpu.VMEM((parts * order, order), BF16)
    home = jax.ShapeDtypeStruct((2, slices, parts, order, width), BF16)
    dma = pltpu.SemaphoreType.DMA
    forward, backward = pl.pallas_call(
        functools.partial(kernel, n_tm, n_col),
        out_shape=(home, home),
        in_specs=[pl.BlockSpec(memory_space=pl.ANY)] * 3,
        out_specs=[pl.BlockSpec(memory_space=pl.ANY)] * 2,
        scratch_shapes=[
            blocks, blocks, blocks, blocks, blocks, pair, pair, whole, whole,
            dma((n_col,)), dma((n_col,)), dma((n_col,)), dma((2, slices)), dma((2, slices)), dma((2,)), dma((2,)),
            dma((n_col,)), dma((7,)), dma((n_col,)), dma((n_col,)), dma((4,)),
        ],
        compiler_params=pltpu.CompilerParams(
            collective_id=0, has_side_effects=True, vmem_limit_bytes=56 * 1024 * 1024
        ),
    )(near_prop, far_prop, meson)
    terms = [array[s].astype(F32) for array in (forward, backward) for s in range(2)]
    return terms[0] + terms[1] + terms[2] + terms[3]


def solution(mesh):
    spec = P("tm", None, None, "col")
    body = functools.partial(shards, mesh.shape["tm"], mesh.shape["col"])
    return jax.shard_map(body, mesh=mesh, in_specs=(spec, spec, spec), out_specs=spec, check_vma=False)
```

```python
import functools

import jax
import jax.numpy as jnp
from jax import lax
from jax.experimental import pallas as pl
from jax.experimental.pallas import tpu as pltpu
from jax.sharding import PartitionSpec as P

MESH = pl.DeviceIdType.MESH
BF16 = jnp.bfloat16
F32 = jnp.float32


def left_form(real, imag):
    top = jnp.concatenate([real, -imag], axis=1)
    low = jnp.concatenate([imag, real], axis=1)
    return jnp.concatenate([top, low], axis=0)


def from_blocks(blocks):
    count = blocks.shape[0]
    real = jnp.concatenate([blocks[j, 0] for j in range(count)], axis=1)
    imag = jnp.concatenate([blocks[j, 1] for j in range(count)], axis=1)
    return left_form(real, imag)


def kernel(
    n_tm, n_col, near, far, meson, f_in, b_in,
    p_in, m_in, a_in, b_out, f_out, bf_in, p_nat, t_nat,
    p_sem, m_sem, a_sem, b_sem, f_sem, bf_sem, p_send, m_send, a_send, b_send, f_send,
):
    order = near.shape[2]
    width = near.shape[3]
    half = order // 2
    tm = lax.axis_index("tm")
    me = lax.axis_index("col")
    y, c = me // 2, me % 2
    step_near, step_far = n_tm // 8, 3 * n_tm // 8
    partner = 2 * y + 1 - c
    across = 2 * (1 - y) + c
    beyond = 2 * (1 - y) + 1 - c
    between = step_far - step_near
    tile = 2 * width

    def shifted(by):
        return lax.rem(tm + by + n_tm, n_tm)

    barrier = pltpu.get_barrier_semaphore()
    steps = (step_near, between)
    for d in range(1, n_col):
        pl.semaphore_signal(barrier, inc=1, device_id=(tm, lax.rem(me + d, n_col)), device_id_type=MESH)
    for step in steps:
        for by in (step, -step):
            for j in range(n_col):
                pl.semaphore_signal(barrier, inc=1, device_id=(shifted(by), j), device_id_type=MESH)
    pl.semaphore_wait(barrier, n_col - 1 + 2 * len(steps) * n_col)

    def remote(src, dst, send, recv, device):
        return pltpu.make_async_remote_copy(
            src_ref=src, dst_ref=dst, send_sem=send, recv_sem=recv, device_id=device, device_id_type=MESH
        )

    def arrived(buf, sem, j):
        pltpu.make_async_copy(buf.at[j], buf.at[j], sem.at[j]).wait()

    def ahead_near(src, j, k):
        device = (shifted(-step_near), 2 * y)
        return remote(src, a_in.at[j], m_send.at[k], a_sem.at[j], device)

    def ahead_far(j):
        device = (shifted(-between), 2 * y + 1)
        return remote(a_in.at[j], a_in.at[j], a_send.at[j], a_sem.at[j], device)

    def to_partner(src, j, k):
        return remote(src, m_in.at[j], m_send.at[2 + k], m_sem.at[j], (tm, partner))

    def spread(src, j, k):
        ahead_near(src, j, k).start()
        to_partner(src, j, k).start()

    def p_copy(target):
        src = (near, far)[target % 2].at[target // 2]
        return remote(src, p_in.at[me], p_send.at[target], p_sem.at[me], (tm, target))

    cross = remote(meson.at[1 - y], m_in.at[me], m_send.at[4], m_sem.at[me], (tm, across))
    cross.start()
    spread(meson.at[y], me, 0)
    pltpu.make_async_copy(meson.at[y], m_in.at[me], m_sem.at[me]).start()
    for target in range(n_col):
        @pl.when(me != target)
        def _():
            p_copy(target).start()

        @pl.when(me == target)
        def _():
            src = (near, far)[target % 2].at[target // 2]
            pltpu.make_async_copy(src, p_in.at[me], p_sem.at[me]).start()

    rows = lax.broadcasted_iota(jnp.int32, (order, width), 0)

    def prepare(j):
        arrived(p_in, p_sem, j)
        first = pl.multiple_of(j * width, width)
        columns = lax.broadcasted_iota(jnp.int32, (order, width), 1) + j * width
        sign = jnp.where((rows < half) == (columns < half), 1.0, -1.0).astype(F32)
        for part in range(2):
            block = p_in[j, part]
            p_nat[part * order:(part + 1) * order, pl.ds(first, width)] = block
            signed = block.astype(F32) * (sign if part == 0 else -sign)
            t_nat[pl.ds(part * order + first, width), :] = jnp.transpose(signed).astype(BF16)

    prepare(me)
    prepare(partner)
    arrived(m_in, m_sem, across)
    spread(m_in.at[across], across, 1)

    @pl.when(c == 0)
    def _():
        for j in (me, partner, across, beyond):
            arrived(a_in, a_sem, j)
            ahead_far(j).start()

    prepare(across)
    prepare(beyond)
    for j in (me, partner, beyond):
        arrived(m_in, m_sem, j)

    def product(left, right):
        return jnp.dot(left, right, preferred_element_type=F32).astype(BF16)

    def store(ref, i, value):
        for k in range(2):
            for part in range(2):
                ref[2 * i + k, part] = value[part * order:(part + 1) * order, k * width:(k + 1) * width]

    def b_far(j):
        return remote(b_out.at[j], bf_in.at[j], b_send.at[j], bf_sem.at[j], (shifted(between), 2 * y))

    def b_home(j):
        return remote(b_out.at[j], b_in.at[y], b_send.at[j], b_sem.at[y], (shifted(step_near), j))

    for i in range(order // tile):
        at = pl.ds(i * tile, tile)
        inner = product(from_blocks(m_in), t_nat[:, at])
        store(b_out, i, product(from_blocks(p_in), inner))

        @pl.when(c == 1)
        def _():
            for j in (2 * i, 2 * i + 1):
                b_far(j).start()

    @pl.when(c == 1)
    def _():
        for j in range(n_col):
            arrived(a_in, a_sem, j)

    def f_copy(target):
        return remote(f_out.at[target], f_in.at[c, y], f_send.at[target], f_sem.at[c, y], (tm, target))

    for i in range(order // tile):
        at = pl.ds(i * tile, tile)
        ahead = product(from_blocks(a_in), p_nat[:, at])
        store(f_out, i, product(left_form(t_nat[:order, :], t_nat[order:, :]), ahead))
        for target in (2 * i, 2 * i + 1):
            @pl.when(me != target)
            def _():
                f_copy(target).start()

            @pl.when(me == target)
            def _():
                pltpu.make_async_copy(f_out.at[target], f_in.at[c, y], f_sem.at[c, y]).start()

    @pl.when(c == 0)
    def _():
        for j in range(n_col):
            arrived(bf_in, bf_sem, j)
            b_out[j] = (b_out[j].astype(F32) + bf_in[j].astype(F32)).astype(BF16)
            b_home(j).start()

    for p in range(2):
        for s in range(2):
            pltpu.make_async_copy(f_in.at[s, p], f_in.at[s, p], f_sem.at[s, p]).wait()
        arrived(b_in, b_sem, p)

    cross.wait_send()
    for k in range(2):
        src, j = ((meson.at[y], me), (m_in.at[across], across))[k]
        ahead_near(src, j, k).wait_send()
        to_partner(src, j, k).wait_send()

    @pl.when(c == 0)
    def _():
        for j in range(n_col):
            ahead_far(j).wait_send()
            b_home(j).wait_send()

    @pl.when(c == 1)
    def _():
        for j in range(n_col):
            b_far(j).wait_send()

    for target in range(n_col):
        @pl.when(me != target)
        def _():
            p_copy(target).wait_send()
            f_copy(target).wait_send()


def shards(n_tm, n_col, near_prop, far_prop, meson):
    slices, parts, order, width = meson.shape
    blocks = pltpu.VMEM((n_col, parts, order, width), BF16)
    whole = pltpu.VMEM((parts * order, order), BF16)
    home = jax.ShapeDtypeStruct((slices, parts, order, width), BF16)
    homes = jax.ShapeDtypeStruct((2, slices, parts, order, width), BF16)
    dma = pltpu.SemaphoreType.DMA
    forward, backward = pl.pallas_call(
        functools.partial(kernel, n_tm, n_col),
        out_shape=(homes, home),
        in_specs=[pl.BlockSpec(memory_space=pl.ANY)] * 3,
        out_specs=[pl.BlockSpec(memory_space=pl.ANY)] * 2,
        scratch_shapes=[
            blocks, blocks, blocks, blocks, blocks, blocks, whole, whole,
            dma((n_col,)), dma((n_col,)), dma((n_col,)), dma((slices,)), dma((2, slices)), dma((n_col,)),
            dma((n_col,)), dma((5,)), dma((n_col,)), dma((n_col,)), dma((n_col,)),
        ],
        compiler_params=pltpu.CompilerParams(
            collective_id=0, has_side_effects=True, vmem_limit_bytes=56 * 1024 * 1024
        ),
    )(near_prop, far_prop, meson)
    return forward[0].astype(F32) + forward[1].astype(F32) + backward.astype(F32)


def solution(mesh):
    spec = P("tm", None, None, "col")
    body = functools.partial(shards, mesh.shape["tm"], mesh.shape["col"])
    return jax.shard_map(body, mesh=mesh, in_specs=(spec, spec, spec), out_specs=spec, check_vma=False)
```

```python
import functools

import jax
import jax.numpy as jnp
from jax import lax
from jax.experimental import pallas as pl
from jax.experimental.pallas import tpu as pltpu
from jax.sharding import PartitionSpec as P

MESH = pl.DeviceIdType.MESH
BF16 = jnp.bfloat16
F32 = jnp.float32


def left_form(real, imag):
    top = jnp.concatenate([real, -imag], axis=1)
    low = jnp.concatenate([imag, real], axis=1)
    return jnp.concatenate([top, low], axis=0)


def from_blocks(blocks):
    count = blocks.shape[0]
    real = jnp.concatenate([blocks[j, 0] for j in range(count)], axis=1)
    imag = jnp.concatenate([blocks[j, 1] for j in range(count)], axis=1)
    return left_form(real, imag)


def kernel(
    n_tm, n_col, near, far, meson, f_in, b_in,
    p_in, m_in, a_in, b_out, f_out, bf_in, p_nat, t_nat,
    p_sem, m_sem, a_sem, b_sem, f_sem, bf_sem, p_send, m_send, a_send, b_send, f_send,
):
    order = near.shape[2]
    width = near.shape[3]
    half = order // 2
    tm = lax.axis_index("tm")
    me = lax.axis_index("col")
    y, c = me // 2, me % 2
    step_near, step_far = n_tm // 8, 3 * n_tm // 8
    partner = 2 * y + 1 - c
    across = 2 * (1 - y) + c
    beyond = 2 * (1 - y) + 1 - c
    between = step_far - step_near
    tile = 2 * width

    def shifted(by):
        return lax.rem(tm + by + n_tm, n_tm)

    barrier = pltpu.get_barrier_semaphore()
    steps = (step_near, between)
    for d in range(1, n_col):
        pl.semaphore_signal(barrier, inc=1, device_id=(tm, lax.rem(me + d, n_col)), device_id_type=MESH)
    for step in steps:
        for by in (step, -step):
            for j in range(n_col):
                pl.semaphore_signal(barrier, inc=1, device_id=(shifted(by), j), device_id_type=MESH)
    pl.semaphore_wait(barrier, n_col - 1 + 2 * len(steps) * n_col)

    def remote(src, dst, send, recv, device):
        return pltpu.make_async_remote_copy(
            src_ref=src, dst_ref=dst, send_sem=send, recv_sem=recv, device_id=device, device_id_type=MESH
        )

    def arrived(buf, sem, j):
        pltpu.make_async_copy(buf.at[j], buf.at[j], sem.at[j]).wait()

    def ahead_near(src, j, k):
        device = (shifted(-step_near), 2 * y)
        return remote(src, a_in.at[j], m_send.at[k], a_sem.at[j], device)

    def ahead_far(j):
        device = (shifted(-between), 2 * y + 1)
        return remote(a_in.at[j], a_in.at[j], a_send.at[j], a_sem.at[j], device)

    def to_partner(src, j, k):
        return remote(src, m_in.at[j], m_send.at[2 + k], m_sem.at[j], (tm, partner))

    def spread(src, j, k):
        ahead_near(src, j, k).start()
        to_partner(src, j, k).start()

    def p_copy(target):
        src = (near, far)[target % 2].at[target // 2]
        return remote(src, p_in.at[me], p_send.at[target], p_sem.at[me], (tm, target))

    cross = remote(meson.at[1 - y], m_in.at[me], m_send.at[4], m_sem.at[me], (tm, across))
    cross.start()
    spread(meson.at[y], me, 0)
    pltpu.make_async_copy(meson.at[y], m_in.at[me], m_sem.at[me]).start()
    for target in tuple(range(1, n_col, 2)) + tuple(range(0, n_col, 2)):
        @pl.when(me != target)
        def _():
            p_copy(target).start()

        @pl.when(me == target)
        def _():
            src = (near, far)[target % 2].at[target // 2]
            pltpu.make_async_copy(src, p_in.at[me], p_sem.at[me]).start()

    rows = lax.broadcasted_iota(jnp.int32, (order, width), 0)

    def prepare(j):
        arrived(p_in, p_sem, j)
        first = pl.multiple_of(j * width, width)
        columns = lax.broadcasted_iota(jnp.int32, (order, width), 1) + j * width
        sign = jnp.where((rows < half) == (columns < half), 1.0, -1.0).astype(F32)
        for part in range(2):
            block = p_in[j, part]
            p_nat[part * order:(part + 1) * order, pl.ds(first, width)] = block
            signed = block.astype(F32) * (sign if part == 0 else -sign)
            t_nat[pl.ds(part * order + first, width), :] = jnp.transpose(signed).astype(BF16)

    prepare(me)
    prepare(partner)
    arrived(m_in, m_sem, across)
    spread(m_in.at[across], across, 1)

    @pl.when(c == 0)
    def _():
        for j in (me, partner, across, beyond):
            arrived(a_in, a_sem, j)
            ahead_far(j).start()

    prepare(across)
    prepare(beyond)
    for j in (me, partner, beyond):
        arrived(m_in, m_sem, j)

    def product(left, right):
        return jnp.dot(left, right, preferred_element_type=F32).astype(BF16)

    def store(ref, i, value):
        for k in range(2):
            for part in range(2):
                ref[2 * i + k, part] = value[part * order:(part + 1) * order, k * width:(k + 1) * width]

    def b_far(j):
        return remote(b_out.at[j], bf_in.at[j], b_send.at[j], bf_sem.at[j], (shifted(between), 2 * y))

    def b_home(j):
        return remote(b_out.at[j], b_in.at[y], b_send.at[j], b_sem.at[y], (shifted(step_near), j))

    for i in range(order // tile):
        at = pl.ds(i * tile, tile)
        inner = product(from_blocks(m_in), t_nat[:, at])
        store(b_out, i, product(from_blocks(p_in), inner))

        @pl.when(c == 1)
        def _():
            for j in (2 * i, 2 * i + 1):
                b_far(j).start()

    def join(blocks):
        @pl.when(c == 0)
        def _():
            for j in blocks:
                arrived(bf_in, bf_sem, j)
                b_out[j] = (b_out[j].astype(F32) + bf_in[j].astype(F32)).astype(BF16)
                b_home(j).start()

    join((0, 1))

    @pl.when(c == 1)
    def _():
        for j in range(n_col):
            arrived(a_in, a_sem, j)

    def f_copy(target):
        return remote(f_out.at[target], f_in.at[c, y], f_send.at[target], f_sem.at[c, y], (tm, target))

    for i in range(order // tile):
        at = pl.ds(i * tile, tile)
        ahead = product(from_blocks(a_in), p_nat[:, at])
        store(f_out, i, product(left_form(t_nat[:order, :], t_nat[order:, :]), ahead))
        for target in (2 * i, 2 * i + 1):
            @pl.when(me != target)
            def _():
                f_copy(target).start()

            @pl.when(me == target)
            def _():
                pltpu.make_async_copy(f_out.at[target], f_in.at[c, y], f_sem.at[c, y]).start()

        join((2 + i,))

    for p in range(2):
        for s in range(2):
            pltpu.make_async_copy(f_in.at[s, p], f_in.at[s, p], f_sem.at[s, p]).wait()
        arrived(b_in, b_sem, p)

    cross.wait_send()
    for k in range(2):
        src, j = ((meson.at[y], me), (m_in.at[across], across))[k]
        ahead_near(src, j, k).wait_send()
        to_partner(src, j, k).wait_send()

    @pl.when(c == 0)
    def _():
        for j in range(n_col):
            ahead_far(j).wait_send()
            b_home(j).wait_send()

    @pl.when(c == 1)
    def _():
        for j in range(n_col):
            b_far(j).wait_send()

    for target in range(n_col):
        @pl.when(me != target)
        def _():
            p_copy(target).wait_send()
            f_copy(target).wait_send()


def shards(n_tm, n_col, near_prop, far_prop, meson):
    slices, parts, order, width = meson.shape
    blocks = pltpu.VMEM((n_col, parts, order, width), BF16)
    whole = pltpu.VMEM((parts * order, order), BF16)
    home = jax.ShapeDtypeStruct((slices, parts, order, width), BF16)
    homes = jax.ShapeDtypeStruct((2, slices, parts, order, width), BF16)
    dma = pltpu.SemaphoreType.DMA
    forward, backward = pl.pallas_call(
        functools.partial(kernel, n_tm, n_col),
        out_shape=(homes, home),
        in_specs=[pl.BlockSpec(memory_space=pl.ANY)] * 3,
        out_specs=[pl.BlockSpec(memory_space=pl.ANY)] * 2,
        scratch_shapes=[
            blocks, blocks, blocks, blocks, blocks, blocks, whole, whole,
            dma((n_col,)), dma((n_col,)), dma((n_col,)), dma((slices,)), dma((2, slices)), dma((n_col,)),
            dma((n_col,)), dma((5,)), dma((n_col,)), dma((n_col,)), dma((n_col,)),
        ],
        compiler_params=pltpu.CompilerParams(
            collective_id=0, has_side_effects=True, vmem_limit_bytes=56 * 1024 * 1024
        ),
    )(near_prop, far_prop, meson)
    return forward[0].astype(F32) + forward[1].astype(F32) + backward.astype(F32)


def solution(mesh):
    spec = P("tm", None, None, "col")
    body = functools.partial(shards, mesh.shape["tm"], mesh.shape["col"])
    return jax.shard_map(body, mesh=mesh, in_specs=(spec, spec, spec), out_specs=spec, check_vma=False)
```

```python
import functools

import jax
import jax.numpy as jnp
from jax import lax
from jax.experimental import pallas as pl
from jax.experimental.pallas import tpu as pltpu
from jax.sharding import PartitionSpec as P

MESH = pl.DeviceIdType.MESH
BF16 = jnp.bfloat16
F32 = jnp.float32


def left_form(real, imag):
    top = jnp.concatenate([real, -imag], axis=1)
    low = jnp.concatenate([imag, real], axis=1)
    return jnp.concatenate([top, low], axis=0)


def from_blocks(blocks):
    count = blocks.shape[0]
    real = jnp.concatenate([blocks[j, 0] for j in range(count)], axis=1)
    imag = jnp.concatenate([blocks[j, 1] for j in range(count)], axis=1)
    return left_form(real, imag)


def kernel(
    n_tm, n_col, near, far, meson, f_in, b_in,
    p_in, m_in, a_in, b_out, f_out, bf_in, p_nat, t_nat,
    p_sem, m_sem, a_sem, b_sem, f_sem, bf_sem, p_send, m_send, a_send, b_send, f_send,
):
    order = near.shape[2]
    width = near.shape[3]
    half = order // 2
    tm = lax.axis_index("tm")
    me = lax.axis_index("col")
    y, c = me // 2, me % 2
    step_near, step_far = n_tm // 8, 3 * n_tm // 8
    partner = 2 * y + 1 - c
    across = 2 * (1 - y) + c
    beyond = 2 * (1 - y) + 1 - c
    between = step_far - step_near
    odd = step_near % 2 == 1
    at_x0, at_x1 = tm % 2 == 0, tm % 2 == 1
    tile = 2 * width

    def shifted(by):
        return lax.rem(tm + by + n_tm, n_tm)

    barrier = pltpu.get_barrier_semaphore()
    steps = (step_near, between) + ((step_far,) if odd else ())
    for d in range(1, n_col):
        pl.semaphore_signal(barrier, inc=1, device_id=(tm, lax.rem(me + d, n_col)), device_id_type=MESH)
    for step in steps:
        for by in (step, -step):
            for j in range(n_col):
                pl.semaphore_signal(barrier, inc=1, device_id=(shifted(by), j), device_id_type=MESH)
    pl.semaphore_wait(barrier, n_col - 1 + 2 * len(steps) * n_col)

    def remote(src, dst, send, recv, device):
        return pltpu.make_async_remote_copy(
            src_ref=src, dst_ref=dst, send_sem=send, recv_sem=recv, device_id=device, device_id_type=MESH
        )

    def arrived(buf, sem, j):
        pltpu.make_async_copy(buf.at[j], buf.at[j], sem.at[j]).wait()

    def ahead_near(src, j, k):
        device = (shifted(-step_near), 2 * y)
        return remote(src, a_in.at[j], m_send.at[k], a_sem.at[j], device)

    def ahead_far(j):
        device = (shifted(-between), 2 * y + 1)
        return remote(a_in.at[j], a_in.at[j], a_send.at[j], a_sem.at[j], device)

    def ahead_direct():
        device = (shifted(-step_far), 2 * y + 1)
        return remote(meson.at[y], a_in.at[me], m_send.at[5], a_sem.at[me], device)

    def to_partner(src, j, k):
        return remote(src, m_in.at[j], m_send.at[2 + k], m_sem.at[j], (tm, partner))

    def spread(src, j, k):
        ahead_near(src, j, k).start()
        to_partner(src, j, k).start()

    def p_copy(target):
        src = (near, far)[target % 2].at[target // 2]
        return remote(src, p_in.at[me], p_send.at[target], p_sem.at[me], (tm, target))

    cross = remote(meson.at[1 - y], m_in.at[me], m_send.at[4], m_sem.at[me], (tm, across))
    cross.start()
    spread(meson.at[y], me, 0)
    if odd:
        @pl.when(at_x1)
        def _():
            ahead_direct().start()

    pltpu.make_async_copy(meson.at[y], m_in.at[me], m_sem.at[me]).start()
    for target in tuple(range(1, n_col, 2)) + tuple(range(0, n_col, 2)):
        @pl.when(me != target)
        def _():
            p_copy(target).start()

        @pl.when(me == target)
        def _():
            src = (near, far)[target % 2].at[target // 2]
            pltpu.make_async_copy(src, p_in.at[me], p_sem.at[me]).start()

    rows = lax.broadcasted_iota(jnp.int32, (order, width), 0)

    def prepare(j):
        arrived(p_in, p_sem, j)
        first = pl.multiple_of(j * width, width)
        columns = lax.broadcasted_iota(jnp.int32, (order, width), 1) + j * width
        sign = jnp.where((rows < half) == (columns < half), 1.0, -1.0).astype(F32)
        for part in range(2):
            block = p_in[j, part]
            p_nat[part * order:(part + 1) * order, pl.ds(first, width)] = block
            signed = block.astype(F32) * (sign if part == 0 else -sign)
            t_nat[pl.ds(part * order + first, width), :] = jnp.transpose(signed).astype(BF16)

    prepare(me)
    prepare(partner)
    arrived(m_in, m_sem, across)
    spread(m_in.at[across], across, 1)

    @pl.when(c == 0)
    def _():
        for j in (me, partner):
            arrived(a_in, a_sem, j)
            if odd:
                @pl.when(at_x1)
                def _():
                    ahead_far(j).start()
            else:
                ahead_far(j).start()
        for j in (across, beyond):
            arrived(a_in, a_sem, j)
            ahead_far(j).start()

    prepare(across)
    prepare(beyond)
    for j in (me, partner, beyond):
        arrived(m_in, m_sem, j)

    def product(left, right):
        return jnp.dot(left, right, preferred_element_type=F32).astype(BF16)

    def store(ref, i, value):
        for k in range(2):
            for part in range(2):
                ref[2 * i + k, part] = value[part * order:(part + 1) * order, k * width:(k + 1) * width]

    def b_far(j):
        return remote(b_out.at[j], bf_in.at[j], b_send.at[j], bf_sem.at[j], (shifted(between), 2 * y))

    def b_home(j):
        return remote(b_out.at[j], b_in.at[y], b_send.at[j], b_sem.at[y], (shifted(step_near), j))

    for i in range(order // tile):
        at = pl.ds(i * tile, tile)
        inner = product(from_blocks(m_in), t_nat[:, at])
        store(b_out, i, product(from_blocks(p_in), inner))

        @pl.when(c == 1)
        def _():
            for j in (2 * i, 2 * i + 1):
                b_far(j).start()

    def join(blocks):
        @pl.when(c == 0)
        def _():
            for j in blocks:
                arrived(bf_in, bf_sem, j)
                b_out[j] = (b_out[j].astype(F32) + bf_in[j].astype(F32)).astype(BF16)
                b_home(j).start()


    @pl.when(c == 1)
    def _():
        for j in range(n_col):
            arrived(a_in, a_sem, j)

    def f_copy(target):
        return remote(f_out.at[target], f_in.at[c, y], f_send.at[target], f_sem.at[c, y], (tm, target))

    for i in range(order // tile):
        at = pl.ds(i * tile, tile)
        ahead = product(from_blocks(a_in), p_nat[:, at])
        store(f_out, i, product(left_form(t_nat[:order, :], t_nat[order:, :]), ahead))
        for target in (2 * i, 2 * i + 1):
            @pl.when(me != target)
            def _():
                f_copy(target).start()

            @pl.when(me == target)
            def _():
                pltpu.make_async_copy(f_out.at[target], f_in.at[c, y], f_sem.at[c, y]).start()

        join((0,) if i == 0 else (1, 2, 3))

    for p in range(2):
        for s in range(2):
            pltpu.make_async_copy(f_in.at[s, p], f_in.at[s, p], f_sem.at[s, p]).wait()
        arrived(b_in, b_sem, p)

    cross.wait_send()
    if odd:
        @pl.when(at_x1)
        def _():
            ahead_direct().wait_send()

    for k in range(2):
        src, j = ((meson.at[y], me), (m_in.at[across], across))[k]
        ahead_near(src, j, k).wait_send()
        to_partner(src, j, k).wait_send()

    @pl.when(c == 0)
    def _():
        for j in (me, partner):
            if odd:
                @pl.when(at_x1)
                def _():
                    ahead_far(j).wait_send()
            else:
                ahead_far(j).wait_send()
        for j in (across, beyond):
            ahead_far(j).wait_send()
        for j in range(n_col):
            b_home(j).wait_send()

    @pl.when(c == 1)
    def _():
        for j in range(n_col):
            b_far(j).wait_send()

    for target in range(n_col):
        @pl.when(me != target)
        def _():
            p_copy(target).wait_send()
            f_copy(target).wait_send()


def shards(n_tm, n_col, near_prop, far_prop, meson):
    slices, parts, order, width = meson.shape
    blocks = pltpu.VMEM((n_col, parts, order, width), BF16)
    whole = pltpu.VMEM((parts * order, order), BF16)
    home = jax.ShapeDtypeStruct((slices, parts, order, width), BF16)
    homes = jax.ShapeDtypeStruct((2, slices, parts, order, width), BF16)
    dma = pltpu.SemaphoreType.DMA
    forward, backward = pl.pallas_call(
        functools.partial(kernel, n_tm, n_col),
        out_shape=(homes, home),
        in_specs=[pl.BlockSpec(memory_space=pl.ANY)] * 3,
        out_specs=[pl.BlockSpec(memory_space=pl.ANY)] * 2,
        scratch_shapes=[
            blocks, blocks, blocks, blocks, blocks, blocks, whole, whole,
            dma((n_col,)), dma((n_col,)), dma((n_col,)), dma((slices,)), dma((2, slices)), dma((n_col,)),
            dma((n_col,)), dma((6,)), dma((n_col,)), dma((n_col,)), dma((n_col,)),
        ],
        compiler_params=pltpu.CompilerParams(
            collective_id=0, has_side_effects=True, vmem_limit_bytes=56 * 1024 * 1024
        ),
    )(near_prop, far_prop, meson)
    return forward[0].astype(F32) + forward[1].astype(F32) + backward.astype(F32)


def solution(mesh):
    spec = P("tm", None, None, "col")
    body = functools.partial(shards, mesh.shape["tm"], mesh.shape["col"])
    return jax.shard_map(body, mesh=mesh, in_specs=(spec, spec, spec), out_specs=spec, check_vma=False)
```

```python
import functools

import jax
import jax.numpy as jnp
from jax import lax
from jax.experimental import pallas as pl
from jax.experimental.pallas import tpu as pltpu
from jax.sharding import PartitionSpec as P

MESH = pl.DeviceIdType.MESH
BF16 = jnp.bfloat16
F32 = jnp.float32


def left_form(real, imag):
    top = jnp.concatenate([real, -imag], axis=1)
    low = jnp.concatenate([imag, real], axis=1)
    return jnp.concatenate([top, low], axis=0)


def from_blocks(blocks):
    count = blocks.shape[0]
    real = jnp.concatenate([blocks[j, 0] for j in range(count)], axis=1)
    imag = jnp.concatenate([blocks[j, 1] for j in range(count)], axis=1)
    return left_form(real, imag)


def kernel(
    n_tm, n_col, near, far, meson, f_in, b_in,
    p_in, m_in, a_in, b_out, f_out, bf_in, p_nat, t_nat,
    p_sem, m_sem, a_sem, b_sem, f_sem, bf_sem, p_send, m_send, a_send, b_send, f_send,
):
    order = near.shape[2]
    width = near.shape[3]
    half = order // 2
    tm = lax.axis_index("tm")
    me = lax.axis_index("col")
    y, c = me // 2, me % 2
    step_near, step_far = n_tm // 8, 3 * n_tm // 8
    partner = 2 * y + 1 - c
    across = 2 * (1 - y) + c
    beyond = 2 * (1 - y) + 1 - c
    between = step_far - step_near
    tile = 2 * width

    def shifted(by):
        return lax.rem(tm + by + n_tm, n_tm)

    barrier = pltpu.get_barrier_semaphore()
    steps = (step_near, between)
    for d in range(1, n_col):
        pl.semaphore_signal(barrier, inc=1, device_id=(tm, lax.rem(me + d, n_col)), device_id_type=MESH)
    for step in steps:
        for by in (step, -step):
            for j in range(n_col):
                pl.semaphore_signal(barrier, inc=1, device_id=(shifted(by), j), device_id_type=MESH)
    pl.semaphore_wait(barrier, n_col - 1 + 2 * len(steps) * n_col)

    def remote(src, dst, send, recv, device):
        return pltpu.make_async_remote_copy(
            src_ref=src, dst_ref=dst, send_sem=send, recv_sem=recv, device_id=device, device_id_type=MESH
        )

    def arrived(buf, sem, j):
        pltpu.make_async_copy(buf.at[j], buf.at[j], sem.at[j]).wait()

    def ahead_near(src, j, k):
        device = (shifted(-step_near), 2 * y)
        return remote(src, a_in.at[j], m_send.at[k], a_sem.at[j], device)

    def ahead_far(j):
        device = (shifted(-between), 2 * y + 1)
        return remote(a_in.at[j], a_in.at[j], a_send.at[j], a_sem.at[j], device)

    def to_partner(src, j, k):
        return remote(src, m_in.at[j], m_send.at[2 + k], m_sem.at[j], (tm, partner))

    def spread(src, j, k):
        ahead_near(src, j, k).start()
        to_partner(src, j, k).start()

    def p_copy(target):
        src = (near, far)[target % 2].at[target // 2]
        return remote(src, p_in.at[me], p_send.at[target], p_sem.at[me], (tm, target))

    cross = remote(meson.at[1 - y], m_in.at[me], m_send.at[4], m_sem.at[me], (tm, across))
    cross.start()
    spread(meson.at[y], me, 0)
    pltpu.make_async_copy(meson.at[y], m_in.at[me], m_sem.at[me]).start()
    for target in tuple(range(1, n_col, 2)) + tuple(range(0, n_col, 2)):
        @pl.when(me != target)
        def _():
            p_copy(target).start()

        @pl.when(me == target)
        def _():
            src = (near, far)[target % 2].at[target // 2]
            pltpu.make_async_copy(src, p_in.at[me], p_sem.at[me]).start()

    rows = lax.broadcasted_iota(jnp.int32, (order, width), 0)

    def prepare(j):
        arrived(p_in, p_sem, j)
        first = pl.multiple_of(j * width, width)
        columns = lax.broadcasted_iota(jnp.int32, (order, width), 1) + j * width
        sign = jnp.where((rows < half) == (columns < half), 1.0, -1.0).astype(F32)
        for part in range(2):
            block = p_in[j, part]
            p_nat[part * order:(part + 1) * order, pl.ds(first, width)] = block
            signed = block.astype(F32) * (sign if part == 0 else -sign)
            t_nat[pl.ds(part * order + first, width), :] = jnp.transpose(signed).astype(BF16)

    prepare(me)
    prepare(partner)
    arrived(m_in, m_sem, across)
    spread(m_in.at[across], across, 1)

    @pl.when(c == 0)
    def _():
        for j in (me, partner, across, beyond):
            arrived(a_in, a_sem, j)
            ahead_far(j).start()

    prepare(across)
    prepare(beyond)
    for j in (me, partner, beyond):
        arrived(m_in, m_sem, j)

    def product(left, right):
        return jnp.dot(left, right, preferred_element_type=F32).astype(BF16)

    def store(ref, i, value):
        for k in range(2):
            for part in range(2):
                ref[2 * i + k, part] = value[part * order:(part + 1) * order, k * width:(k + 1) * width]

    def b_far(j):
        return remote(b_out.at[j], bf_in.at[j], b_send.at[j], bf_sem.at[j], (shifted(between), 2 * y))

    def b_home(j):
        return remote(b_out.at[j], b_in.at[y], b_send.at[j], b_sem.at[y], (shifted(step_near), j))

    for i in range(order // tile):
        at = pl.ds(i * tile, tile)
        inner = product(from_blocks(m_in), t_nat[:, at])
        store(b_out, i, product(from_blocks(p_in), inner))

        @pl.when(c == 1)
        def _():
            for j in (2 * i, 2 * i + 1):
                b_far(j).start()

    def join(blocks):
        @pl.when(c == 0)
        def _():
            for j in blocks:
                arrived(bf_in, bf_sem, j)
                b_out[j] = (b_out[j].astype(F32) + bf_in[j].astype(F32)).astype(BF16)
                b_home(j).start()


    @pl.when(c == 1)
    def _():
        for j in range(n_col):
            arrived(a_in, a_sem, j)

    def f_copy(target):
        return remote(f_out.at[target], f_in.at[c, y], f_send.at[target], f_sem.at[c, y], (tm, target))

    for i in range(order // tile):
        at = pl.ds(i * tile, tile)
        ahead = product(from_blocks(a_in), p_nat[:, at])
        store(f_out, i, product(left_form(t_nat[:order, :], t_nat[order:, :]), ahead))
        for target in (2 * i, 2 * i + 1):
            @pl.when(me != target)
            def _():
                f_copy(target).start()

            @pl.when(me == target)
            def _():
                pltpu.make_async_copy(f_out.at[target], f_in.at[c, y], f_sem.at[c, y]).start()

        join((0,) if i == 0 else (1, 2, 3))

    for p in range(2):
        for s in range(2):
            pltpu.make_async_copy(f_in.at[s, p], f_in.at[s, p], f_sem.at[s, p]).wait()
        arrived(b_in, b_sem, p)

    cross.wait_send()
    for k in range(2):
        src, j = ((meson.at[y], me), (m_in.at[across], across))[k]
        ahead_near(src, j, k).wait_send()
        to_partner(src, j, k).wait_send()

    @pl.when(c == 0)
    def _():
        for j in range(n_col):
            ahead_far(j).wait_send()
            b_home(j).wait_send()

    @pl.when(c == 1)
    def _():
        for j in range(n_col):
            b_far(j).wait_send()

    for target in range(n_col):
        @pl.when(me != target)
        def _():
            p_copy(target).wait_send()
            f_copy(target).wait_send()


def shards(n_tm, n_col, near_prop, far_prop, meson):
    slices, parts, order, width = meson.shape
    blocks = pltpu.VMEM((n_col, parts, order, width), BF16)
    whole = pltpu.VMEM((parts * order, order), BF16)
    home = jax.ShapeDtypeStruct((slices, parts, order, width), BF16)
    homes = jax.ShapeDtypeStruct((2, slices, parts, order, width), BF16)
    dma = pltpu.SemaphoreType.DMA
    forward, backward = pl.pallas_call(
        functools.partial(kernel, n_tm, n_col),
        out_shape=(homes, home),
        in_specs=[pl.BlockSpec(memory_space=pl.ANY)] * 3,
        out_specs=[pl.BlockSpec(memory_space=pl.ANY)] * 2,
        scratch_shapes=[
            blocks, blocks, blocks, blocks, blocks, blocks, whole, whole,
            dma((n_col,)), dma((n_col,)), dma((n_col,)), dma((slices,)), dma((2, slices)), dma((n_col,)),
            dma((n_col,)), dma((5,)), dma((n_col,)), dma((n_col,)), dma((n_col,)),
        ],
        compiler_params=pltpu.CompilerParams(
            collective_id=0, has_side_effects=True, vmem_limit_bytes=56 * 1024 * 1024
        ),
    )(near_prop, far_prop, meson)
    return forward[0].astype(F32) + forward[1].astype(F32) + backward.astype(F32)


def solution(mesh):
    spec = P("tm", None, None, "col")
    body = functools.partial(shards, mesh.shape["tm"], mesh.shape["col"])
    return jax.shard_map(body, mesh=mesh, in_specs=(spec, spec, spec), out_specs=spec, check_vma=False)
```
